512 devices in a mesh: seq: 512 (over x, z, y, core).
Axes of the slice: x: 4, y: 4, z: 16, core: 2. Of those that a mesh axis runs over, the one named last changes fastest.
Arguments:
- signal: bfloat16 [524288, 512], P('seq'), may hold values from -6 to 6
- grad_out: bfloat16 [524288, 512], P('seq'), may hold values from -6 to 6
- conv_weight: bfloat16 [1024, 1024], replicated, may hold values from -0.1875 to 0.1875
- proj_weight: bfloat16 [512, 512], replicated, may hold values from -0.25 to 0.25
Outputs:
- saliency: float32 [524288, 512], P('seq')
The draws below stay inside these ranges and needn't reach their ends.
All inputs are finite; a program needn't handle non-finite values.
Results may differ from the reference program's by a relative error of at most 0.0013.
Values may be sent and summed in bfloat16 or wider, within the bound.
No kernel may reach another device: no remote copies, remote signals or barrier semaphores. Data moves between devices by JAX's collectives and lax.ppermute only.
A program may use at most 64 MiB of HBM per device.

```python
import jax
import jax.numpy as jnp
from jax import lax

C = 512
GATE = 1024
TOTAL = 524288
DILATION = 2048


def shard_levels(rng, extent, pieces, smallest, largest):
    def one(axis_at, blocks):
        steps = jax.random.uniform(jax.random.fold_in(jax.random.fold_in(rng, 6), axis_at), (blocks,), jnp.float32, smallest / len(pieces), largest / len(pieces))
        return jnp.repeat(jnp.exp(steps), extent[axis_at] // blocks).reshape((-1,) + (1,) * (len(extent) - axis_at - 1))

    gain = one(*pieces[0])
    for cut in pieces[1:]:
        gain = gain * one(*cut)
    return gain


def bell_draw(own_key, dims, width, limit, pieces=(), dtype=jnp.bfloat16):
    gain = shard_levels(own_key, dims, pieces, -0.22, 0.18) if pieces else 1.0
    entries = jax.random.normal(own_key, dims, jnp.float32) * width * gain
    return jnp.minimum(jnp.maximum(entries, -limit), limit).astype(dtype)


def setup_inputs(seed: int = 0) -> dict:
    keys = jax.random.split(jax.random.key(seed), 5)
    signal = bell_draw(keys[0], (TOTAL, C), 1.0, 6.0, ((0, 512),))
    grad_out = bell_draw(keys[1], (TOTAL, C), 1.0, 6.0, ((0, 512),))
    conv_weight = bell_draw(keys[2], (2 * C, GATE), (2 * C) ** -0.5, 0.1875)
    proj_weight = bell_draw(keys[3], (C, C), C ** -0.5, 0.25)
    return {"signal": signal, "grad_out": grad_out, "conv_weight": conv_weight, "proj_weight": proj_weight}


def contract_rows(left, right):
    return lax.dot_general(left, right, (((1,), (1,)), ((), ())), preferred_element_type=jnp.float32)


def reference(signal, grad_out, conv_weight, proj_weight):
    w_past = conv_weight[:C]
    w_now = conv_weight[C:]
    past = jnp.concatenate([jnp.zeros((DILATION, C), jnp.bfloat16), signal[:-DILATION]], 0)
    gates = jnp.dot(past, w_past, preferred_element_type=jnp.float32) + jnp.dot(signal, w_now, preferred_element_type=jnp.float32)
    tanh_part = jnp.tanh(gates[:, :C])
    sig_part = jax.nn.sigmoid(gates[:, C:])
    d_mixed = contract_rows(grad_out, proj_weight)
    d_tanh = d_mixed * sig_part * (1.0 - tanh_part * tanh_part)
    d_sig = d_mixed * tanh_part * sig_part * (1.0 - sig_part)
    d_gates = jnp.concatenate([d_tanh, d_sig], 1).astype(jnp.bfloat16)
    near = contract_rows(d_gates, w_now)
    far = lax.optimization_barrier(contract_rows(d_gates, w_past).astype(jnp.bfloat16))
    back = jnp.concatenate([far[DILATION:], jnp.zeros((DILATION, C), jnp.bfloat16)], 0).astype(jnp.float32)
    return grad_out.astype(jnp.float32) + near + back
```

```python
import jax
import jax.numpy as jnp
from jax import lax
from jax.sharding import PartitionSpec as P

PARTS = 4


def from_behind(block, axis, distance):
    devices = range(lax.axis_size(axis))
    route = [(i - distance, i) for i in devices if i - distance in devices]
    return lax.ppermute(block, axis, route)


def contract_rows(left, right):
    return lax.dot_general(
        left, right, (((1,), (1,)), ((), ())), preferred_element_type=jnp.float32
    )


def shards(signal, grad_out, conv_weight, proj_weight):
    rows, width = signal.shape
    step = rows // PARTS
    w_past = conv_weight[:width]
    w_now = conv_weight[width:]
    cut = lambda a, k: a[k * step : (k + 1) * step]
    past = [from_behind(cut(signal, k), "seq", 2) for k in range(PARTS)]
    outs = []
    for k in range(PARTS):
        own = jnp.dot(cut(signal, k), w_now, preferred_element_type=jnp.float32)
        gates = own + jnp.dot(past[k], w_past, preferred_element_type=jnp.float32)
        tanh_part = jnp.tanh(gates[:, :width])
        sig_part = jax.nn.sigmoid(gates[:, width:])
        d_mixed = contract_rows(cut(grad_out, k), proj_weight)
        d_tanh = d_mixed * sig_part * (1.0 - tanh_part * tanh_part)
        d_sig = d_mixed * tanh_part * sig_part * (1.0 - sig_part)
        d_gates = jnp.concatenate([d_tanh, d_sig], 1).astype(jnp.bfloat16)
        far = contract_rows(d_gates, w_past).astype(jnp.bfloat16)
        back = from_behind(far, "seq", -2).astype(jnp.float32)
        near = contract_rows(d_gates, w_now)
        outs.append(cut(grad_out, k).astype(jnp.float32) + near + back)
    return jnp.concatenate(outs, 0)


def solution(mesh):
    in_specs = (P("seq", None), P("seq", None), P(), P())
    out_specs = P("seq", None)
    return jax.shard_map(shards, mesh=mesh, in_specs=in_specs, out_specs=out_specs, check_vma=False)
```

```python
import jax
import jax.numpy as jnp
from jax import lax
from jax.sharding import PartitionSpec as P


PARTS = (384, 320)
TWICE = 320


def from_behind(block, axis, distance):
    devices = range(lax.axis_size(axis))
    route = [(i - distance, i) for i in devices if i - distance in devices]
    return lax.ppermute(block, axis, route)


def contract_rows(left, right):
    return lax.dot_general(
        left, right, (((1,), (1,)), ((), ())), preferred_element_type=jnp.float32
    )


def shards(signal, grad_out, conv_weight, proj_weight):
    _, width = signal.shape
    w_past = conv_weight[:width]
    w_now = conv_weight[width:]

    def gradients(past, now, grad):
        own = jnp.dot(now, w_now, preferred_element_type=jnp.float32)
        gates = own + jnp.dot(past, w_past, preferred_element_type=jnp.float32)
        tanh_part = jnp.tanh(gates[:, :width])
        sig_part = jax.nn.sigmoid(gates[:, width:])
        d_mixed = contract_rows(grad, proj_weight)
        d_tanh = d_mixed * sig_part * (1.0 - tanh_part * tanh_part)
        d_sig = d_mixed * tanh_part * sig_part * (1.0 - sig_part)
        return jnp.concatenate([d_tanh, d_sig], 1).astype(jnp.bfloat16)

    def far_of(d_gates):
        return contract_rows(d_gates, w_past).astype(jnp.bfloat16)

    both = jnp.concatenate([signal[:TWICE], grad_out[:TWICE]], 0)
    cuts = [(TWICE + sum(PARTS[:k]), TWICE + sum(PARTS[: k + 1])) for k in range(len(PARTS))]
    past = [from_behind(signal[a:b], "seq", 2) for a, b in cuts]
    ahead = from_behind(both, "seq", -2)
    past_both = from_behind(signal[:TWICE], "seq", 2)
    accs = []
    backs = []
    for k, (a, b) in enumerate(cuts):
        d_gates = gradients(past[k], signal[a:b], grad_out[a:b])
        backs.append(from_behind(far_of(d_gates), "seq", -2))
        acc = grad_out[a:b].astype(jnp.float32) + contract_rows(d_gates, w_now)
        accs.append(lax.optimization_barrier(acc))
    far = far_of(gradients(signal[:TWICE], ahead[:TWICE], ahead[TWICE:]))
    d_gates = gradients(past_both, signal[:TWICE], grad_out[:TWICE])
    first = grad_out[:TWICE].astype(jnp.float32) + contract_rows(d_gates, w_now)
    first = lax.optimization_barrier(first + far.astype(jnp.float32))
    mids = [acc + back.astype(jnp.float32) for acc, back in zip(accs[:-1], backs)]
    out = jnp.concatenate([first, *mids, accs[-1]], 0)
    last = accs[-1] + backs[-1].astype(jnp.float32)
    return lax.dynamic_update_slice(out, last, (cuts[-1][0], 0))


def solution(mesh):
    in_specs = (P("seq", None), P("seq", None), P(), P())
    out_specs = P("seq", None)
    return jax.shard_map(shards, mesh=mesh, in_specs=in_specs, out_specs=out_specs, check_vma=False)
```

```python
import functools

import jax
import jax.numpy as jnp
from jax import lax
from jax.experimental import pallas as pl
from jax.experimental.pallas import tpu as pltpu
from jax.sharding import PartitionSpec as P


PARTS = (384, 320)
TWICE = 320


def from_behind(block, axis, distance):
    devices = range(lax.axis_size(axis))
    route = [(i - distance, i) for i in devices if i - distance in devices]
    return lax.ppermute(block, axis, route)


def contract_rows(left, right):
    return lax.dot_general(
        left, right, (((1,), (1,)), ((), ())), preferred_element_type=jnp.float32
    )


def cut_body(pieces, *refs):
    count = len(refs) - 1 - len({o for _, _, o, _, _ in pieces})
    sources, targets, sems = refs[:count], refs[count:-1], refs[-1]
    copies = []
    for k, (source, at, target, to, size) in enumerate(pieces):
        rows = sources[source].at[pl.ds(at, size)]
        copies.append(pltpu.make_async_copy(rows, targets[target].at[pl.ds(to, size)], sems.at[k]))
        copies[-1].start()
    for copy in copies:
        copy.wait()


def cut_rows(arrays, pieces, sizes, space):
    width = arrays[0].shape[1]
    vmem = pl.BlockSpec(memory_space=pltpu.VMEM)
    return pl.pallas_call(
        functools.partial(cut_body, pieces),
        out_shape=[jax.ShapeDtypeStruct((n, width), arrays[0].dtype) for n in sizes],
        in_specs=[pl.BlockSpec(memory_space=space)] * len(arrays),
        out_specs=[vmem] * len(sizes),
        scratch_shapes=[pltpu.SemaphoreType.DMA((len(pieces),))],
        compiler_params=pltpu.CompilerParams(vmem_limit_bytes=2 * 2**20),
    )(*arrays)


def shards(signal, grad_out, conv_weight, proj_weight):
    _, width = signal.shape
    w_past = conv_weight[:width]
    w_now = conv_weight[width:]

    def gradients(past, now, grad):
        own = jnp.dot(now, w_now, preferred_element_type=jnp.float32)
        gates = own + jnp.dot(past, w_past, preferred_element_type=jnp.float32)
        tanh_part = jnp.tanh(gates[:, :width])
        sig_part = jax.nn.sigmoid(gates[:, width:])
        d_mixed = contract_rows(grad, proj_weight)
        d_tanh = d_mixed * sig_part * (1.0 - tanh_part * tanh_part)
        d_sig = d_mixed * tanh_part * sig_part * (1.0 - sig_part)
        return jnp.concatenate([d_tanh, d_sig], 1).astype(jnp.bfloat16)

    def far_of(d_gates):
        return contract_rows(d_gates, w_past).astype(jnp.bfloat16)

    cuts = [(TWICE + sum(PARTS[:k]), TWICE + sum(PARTS[: k + 1])) for k in range(len(PARTS))]
    pieces = ((0, TWICE, 0, 0, PARTS[0]), (0, 0, 1, 0, TWICE), (1, 0, 1, TWICE, TWICE))
    held = [pltpu.with_memory_space_constraint(a, pltpu.HBM) for a in (signal, grad_out)]
    part, both = cut_rows(held, pieces, (PARTS[0], 2 * TWICE), pltpu.HBM)
    past = [from_behind(part, "seq", 2)]
    ahead = from_behind(both, "seq", -2)
    pieces = ((0, cuts[1][0], 0, 0, PARTS[1]), (0, 0, 1, 0, TWICE))
    part, head = cut_rows([signal, grad_out], pieces, (PARTS[1], TWICE), pltpu.VMEM)
    past.append(from_behind(part, "seq", 2))
    past_both = from_behind(head, "seq", 2)
    accs = []
    backs = []
    for k, (a, b) in enumerate(cuts):
        d_gates = gradients(past[k], signal[a:b], grad_out[a:b])
        backs.append(from_behind(far_of(d_gates), "seq", -2))
        acc = grad_out[a:b].astype(jnp.float32) + contract_rows(d_gates, w_now)
        accs.append(lax.optimization_barrier(acc))
    far = far_of(gradients(signal[:TWICE], ahead[:TWICE], ahead[TWICE:]))
    d_gates = gradients(past_both, signal[:TWICE], grad_out[:TWICE])
    first = grad_out[:TWICE].astype(jnp.float32) + contract_rows(d_gates, w_now)
    first = lax.optimization_barrier(first + far.astype(jnp.float32))
    mids = [acc + back.astype(jnp.float32) for acc, back in zip(accs[:-1], backs)]
    out = jnp.concatenate([first, *mids, accs[-1]], 0)
    last = accs[-1] + backs[-1].astype(jnp.float32)
    return lax.dynamic_update_slice(out, last, (cuts[-1][0], 0))


def solution(mesh):
    in_specs = (P("seq", None), P("seq", None), P(), P())
    out_specs = P("seq", None)
    return jax.shard_map(shards, mesh=mesh, in_specs=in_specs, out_specs=out_specs, check_vma=False)
```

```python
import functools

import jax
import jax.numpy as jnp
from jax import lax
from jax.experimental import pallas as pl
from jax.experimental.pallas import tpu as pltpu
from jax.sharding import PartitionSpec as P


PARTS = (352, 320)
TWICE = 352


def from_behind(block, axis, distance):
    devices = range(lax.axis_size(axis))
    route = [(i - distance, i) for i in devices if i - distance in devices]
    return lax.ppermute(block, axis, route)


def contract_rows(left, right):
    return lax.dot_general(
        left, right, (((1,), (1,)), ((), ())), preferred_element_type=jnp.float32
    )


def cut_body(pieces, *refs):
    count = len(refs) - 1 - len({o for _, _, o, _, _ in pieces})
    sources, targets, sems = refs[:count], refs[count:-1], refs[-1]
    copies = []
    for k, (source, at, target, to, size) in enumerate(pieces):
        rows = sources[source].at[pl.ds(at, size)]
        copies.append(pltpu.make_async_copy(rows, targets[target].at[pl.ds(to, size)], sems.at[k]))
        copies[-1].start()
    for copy in copies:
        copy.wait()


def cut_rows(arrays, pieces, sizes, space):
    width = arrays[0].shape[1]
    vmem = pl.BlockSpec(memory_space=pltpu.VMEM)
    return pl.pallas_call(
        functools.partial(cut_body, pieces),
        out_shape=[jax.ShapeDtypeStruct((n, width), arrays[0].dtype) for n in sizes],
        in_specs=[pl.BlockSpec(memory_space=space)] * len(arrays),
        out_specs=[vmem] * len(sizes),
        scratch_shapes=[pltpu.SemaphoreType.DMA((len(pieces),))],
        compiler_params=pltpu.CompilerParams(vmem_limit_bytes=2 * 2**20),
    )(*arrays)


def last_body(start, whole, acc, back, out, held, sems):
    count = sems.shape[0]
    size = acc.shape[0] // count
    copies = []
    for k in range(count):
        r = pl.ds(k * size, size)
        held[r] = acc[r] + back[r].astype(jnp.float32)
        copies.append(pltpu.make_async_copy(held.at[r], out.at[pl.ds(start + k * size, size)], sems.at[k]))
        copies[-1].start()
    for copy in copies:
        copy.wait()


def put_last(whole, acc, back, start):
    vmem, anywhere = (pl.BlockSpec(memory_space=m) for m in (pltpu.VMEM, pl.ANY))
    return pl.pallas_call(
        functools.partial(last_body, start),
        out_shape=jax.ShapeDtypeStruct(whole.shape, whole.dtype),
        in_specs=[anywhere, vmem, vmem],
        out_specs=anywhere,
        scratch_shapes=[pltpu.VMEM(acc.shape, acc.dtype), pltpu.SemaphoreType.DMA((4,))],
        input_output_aliases={0: 0},
        compiler_params=pltpu.CompilerParams(vmem_limit_bytes=4 * 2**20),
        name="put_last",
    )(whole, acc, back)


def shards(signal, grad_out, conv_weight, proj_weight):
    _, width = signal.shape
    w_past = conv_weight[:width]
    w_now = conv_weight[width:]

    def gradients(past, now, grad):
        own = jnp.dot(now, w_now, preferred_element_type=jnp.float32)
        gates = own + jnp.dot(past, w_past, preferred_element_type=jnp.float32)
        tanh_part = jnp.tanh(gates[:, :width])
        sig_part = jax.nn.sigmoid(gates[:, width:])
        d_mixed = contract_rows(grad, proj_weight)
        d_tanh = d_mixed * sig_part * (1.0 - tanh_part * tanh_part)
        d_sig = d_mixed * tanh_part * sig_part * (1.0 - sig_part)
        return jnp.concatenate([d_tanh, d_sig], 1).astype(jnp.bfloat16)

    def far_of(d_gates):
        return contract_rows(d_gates, w_past).astype(jnp.bfloat16)

    cuts = [(TWICE + sum(PARTS[:k]), TWICE + sum(PARTS[: k + 1])) for k in range(len(PARTS))]
    pieces = ((0, TWICE, 0, 0, PARTS[0]), (0, 0, 1, 0, TWICE), (1, 0, 1, TWICE, TWICE))
    held = [pltpu.with_memory_space_constraint(a, pltpu.HBM) for a in (signal, grad_out)]
    part, both = cut_rows(held, pieces, (PARTS[0], 2 * TWICE), pltpu.HBM)
    past = [from_behind(part, "seq", 2)]
    ahead = from_behind(both, "seq", -2)
    pieces = ((0, cuts[1][0], 0, 0, PARTS[1]), (0, 0, 1, 0, TWICE))
    part, head = cut_rows([signal, grad_out], pieces, (PARTS[1], TWICE), pltpu.VMEM)
    past.append(from_behind(part, "seq", 2))
    past_both = from_behind(head, "seq", 2)
    accs = []
    backs = []
    for k, (a, b) in enumerate(cuts):
        d_gates = gradients(past[k], signal[a:b], grad_out[a:b])
        backs.append(from_behind(far_of(d_gates), "seq", -2))
        acc = grad_out[a:b].astype(jnp.float32) + contract_rows(d_gates, w_now)
        accs.append(lax.optimization_barrier(acc))
    far = far_of(gradients(signal[:TWICE], ahead[:TWICE], ahead[TWICE:]))
    d_gates = gradients(past_both, signal[:TWICE], grad_out[:TWICE])
    first = grad_out[:TWICE].astype(jnp.float32) + contract_rows(d_gates, w_now)
    first = lax.optimization_barrier(first + far.astype(jnp.float32))
    mids = [acc + back.astype(jnp.float32) for acc, back in zip(accs[:-1], backs)]
    out = jnp.concatenate([first, *mids, accs[-1]], 0)
    return put_last(out, accs[-1], backs[-1], cuts[-1][0])


def solution(mesh):
    in_specs = (P("seq", None), P("seq", None), P(), P())
    out_specs = P("seq", None)
    return jax.shard_map(shards, mesh=mesh, in_specs=in_specs, out_specs=out_specs, check_vma=False)
```

```python
import functools

import jax
import jax.numpy as jnp
from jax import lax
from jax.experimental import pallas as pl
from jax.experimental.pallas import tpu as pltpu
from jax.sharding import PartitionSpec as P


PARTS = (416, 256)
TWICE = 352
COVER = 10**10


def from_behind(block, axis, distance):
    devices = range(lax.axis_size(axis))
    route = [(i - distance, i) for i in devices if i - distance in devices]
    return lax.ppermute(block, axis, route)


def contract_rows(left, right):
    return lax.dot_general(
        left, right, (((1,), (1,)), ((), ())), preferred_element_type=jnp.float32
    )


def cut_body(pieces, *refs):
    count = len(refs) - 1 - len({o for _, _, o, _, _ in pieces})
    sources, targets, sems = refs[:count], refs[count:-1], refs[-1]
    copies = []
    for k, (source, at, target, to, size) in enumerate(pieces):
        rows = sources[source].at[pl.ds(at, size)]
        copies.append(pltpu.make_async_copy(rows, targets[target].at[pl.ds(to, size)], sems.at[k]))
        copies[-1].start()
    for copy in copies:
        copy.wait()


def cut_rows(arrays, pieces, sizes, space, flops):
    width = arrays[0].shape[1]
    vmem = pl.BlockSpec(memory_space=pltpu.VMEM)
    return pl.pallas_call(
        functools.partial(cut_body, pieces),
        out_shape=[jax.ShapeDtypeStruct((n, width), arrays[0].dtype) for n in sizes],
        in_specs=[pl.BlockSpec(memory_space=space)] * len(arrays),
        out_specs=[vmem] * len(sizes),
        scratch_shapes=[pltpu.SemaphoreType.DMA((len(pieces),))],
        cost_estimate=pl.CostEstimate(flops=flops, bytes_accessed=0, transcendentals=0),
        compiler_params=pltpu.CompilerParams(vmem_limit_bytes=2 * 2**20),
    )(*arrays)


def shards(signal, grad_out, conv_weight, proj_weight):
    _, width = signal.shape
    w_past = conv_weight[:width]
    w_now = conv_weight[width:]

    def gradients(past, now, grad):
        own = jnp.dot(now, w_now, preferred_element_type=jnp.float32)
        gates = own + jnp.dot(past, w_past, preferred_element_type=jnp.float32)
        tanh_part = jnp.tanh(gates[:, :width])
        sig_part = jax.nn.sigmoid(gates[:, width:])
        d_mixed = contract_rows(grad, proj_weight)
        d_tanh = d_mixed * sig_part * (1.0 - tanh_part * tanh_part)
        d_sig = d_mixed * tanh_part * sig_part * (1.0 - sig_part)
        return jnp.concatenate([d_tanh, d_sig], 1).astype(jnp.bfloat16)

    def far_of(d_gates):
        return contract_rows(d_gates, w_past).astype(jnp.bfloat16)

    cuts = [(TWICE + sum(PARTS[:k]), TWICE + sum(PARTS[: k + 1])) for k in range(len(PARTS))]
    pieces = ((0, TWICE, 0, 0, PARTS[0]), (0, 0, 1, 0, TWICE), (1, 0, 1, TWICE, TWICE))
    pieces += ((0, cuts[1][0], 2, 0, PARTS[1]),)
    held = [pltpu.with_memory_space_constraint(a, pltpu.HBM) for a in (signal, grad_out)]
    sizes = (PARTS[0], 2 * TWICE, PARTS[1])
    first_part, both, second_part = cut_rows(held, pieces, sizes, pltpu.HBM, 0)
    parts = (first_part, second_part)
    past = [from_behind(parts[0], "seq", 2)]
    ahead = from_behind(both, "seq", -2)
    (head,) = cut_rows([both], ((0, 0, 0, 0, TWICE),), (TWICE,), pltpu.VMEM, COVER)
    past.append(from_behind(parts[1], "seq", 2))
    past_both = from_behind(head, "seq", 2)
    accs = []
    backs = []
    for k, (a, b) in enumerate(cuts):
        d_gates = gradients(past[k], parts[k], grad_out[a:b])
        backs.append(from_behind(far_of(d_gates), "seq", -2))
        acc = grad_out[a:b].astype(jnp.float32) + contract_rows(d_gates, w_now)
        accs.append(lax.optimization_barrier(acc))
    far = far_of(gradients(both[:TWICE], ahead[:TWICE], ahead[TWICE:]))
    d_gates = gradients(past_both, both[:TWICE], both[TWICE:])
    first = grad_out[:TWICE].astype(jnp.float32) + contract_rows(d_gates, w_now)
    first = lax.optimization_barrier(first + far.astype(jnp.float32))
    mids = [acc + back.astype(jnp.float32) for acc, back in zip(accs[:-1], backs)]
    out = jnp.concatenate([first, *mids, accs[-1]], 0)
    last = accs[-1] + backs[-1].astype(jnp.float32)
    return lax.dynamic_update_slice(out, last, (cuts[-1][0], 0))


def solution(mesh):
    in_specs = (P("seq", None), P("seq", None), P(), P())
    out_specs = P("seq", None)
    return jax.shard_map(shards, mesh=mesh, in_specs=in_specs, out_specs=out_specs, check_vma=False)
```

```python
import functools

import jax
import jax.numpy as jnp
from jax import lax
from jax.experimental import pallas as pl
from jax.experimental.pallas import tpu as pltpu
from jax.sharding import PartitionSpec as P


PARTS = (384, 320)
TWICE = 320
COVER = 10**10


def from_behind(block, axis, distance):
    devices = range(lax.axis_size(axis))
    route = [(i - distance, i) for i in devices if i - distance in devices]
    return lax.ppermute(block, axis, route)


def contract_rows(left, right):
    return lax.dot_general(
        left, right, (((1,), (1,)), ((), ())), preferred_element_type=jnp.float32
    )


def cut_body(pieces, *refs):
    count = len(refs) - 1 - len({o for _, _, o, _, _ in pieces})
    sources, targets, sems = refs[:count], refs[count:-1], refs[-1]
    copies = []
    for k, (source, at, target, to, size) in enumerate(pieces):
        rows = sources[source].at[pl.ds(at, size)]
        copies.append(pltpu.make_async_copy(rows, targets[target].at[pl.ds(to, size)], sems.at[k]))
        copies[-1].start()
    for copy in copies:
        copy.wait()


def cut_rows(arrays, pieces, sizes, space, flops):
    width = arrays[0].shape[1]
    vmem = pl.BlockSpec(memory_space=pltpu.VMEM)
    return pl.pallas_call(
        functools.partial(cut_body, pieces),
        out_shape=[jax.ShapeDtypeStruct((n, width), arrays[0].dtype) for n in sizes],
        in_specs=[pl.BlockSpec(memory_space=space)] * len(arrays),
        out_specs=[vmem] * len(sizes),
        scratch_shapes=[pltpu.SemaphoreType.DMA((len(pieces),))],
        cost_estimate=pl.CostEstimate(flops=flops, bytes_accessed=0, transcendentals=0),
        compiler_params=pltpu.CompilerParams(vmem_limit_bytes=2 * 2**20),
    )(*arrays)


def shards(signal, grad_out, conv_weight, proj_weight):
    _, width = signal.shape
    w_past = conv_weight[:width]
    w_now = conv_weight[width:]

    def gradients(past, now, grad, own=None):
        if own is None:
            own = jnp.dot(now, w_now, preferred_element_type=jnp.float32)
        gates = own + jnp.dot(past, w_past, preferred_element_type=jnp.float32)
        tanh_part = jnp.tanh(gates[:, :width])
        sig_part = jax.nn.sigmoid(gates[:, width:])
        d_mixed = contract_rows(grad, proj_weight)
        d_tanh = d_mixed * sig_part * (1.0 - tanh_part * tanh_part)
        d_sig = d_mixed * tanh_part * sig_part * (1.0 - sig_part)
        return jnp.concatenate([d_tanh, d_sig], 1).astype(jnp.bfloat16)

    def far_of(d_gates):
        return contract_rows(d_gates, w_past).astype(jnp.bfloat16)

    cuts = [(TWICE + sum(PARTS[:k]), TWICE + sum(PARTS[: k + 1])) for k in range(len(PARTS))]
    pieces = ((0, TWICE, 0, 0, PARTS[0]), (0, 0, 1, 0, TWICE), (1, 0, 1, TWICE, TWICE))
    held = [pltpu.with_memory_space_constraint(a, pltpu.HBM) for a in (signal, grad_out)]
    part, both = cut_rows(held, pieces, (PARTS[0], 2 * TWICE), pltpu.HBM, 0)
    past = [from_behind(part, "seq", 2)]
    ahead = from_behind(both, "seq", -2)
    pieces = ((0, cuts[1][0], 0, 0, PARTS[1]), (0, 0, 1, 0, TWICE))
    part, head = cut_rows([signal, grad_out], pieces, (PARTS[1], TWICE), pltpu.VMEM, COVER)
    past.append(from_behind(part, "seq", 2))
    own = jnp.dot(signal[cuts[0][0] : cuts[0][1]], w_now, preferred_element_type=jnp.float32)
    own, head = lax.optimization_barrier((own, head))
    past_both = from_behind(head, "seq", 2)
    accs = []
    backs = []
    for k, (a, b) in enumerate(cuts):
        d_gates = gradients(past[k], signal[a:b], grad_out[a:b], own if k == 0 else None)
        backs.append(from_behind(far_of(d_gates), "seq", -2))
        acc = grad_out[a:b].astype(jnp.float32) + contract_rows(d_gates, w_now)
        accs.append(lax.optimization_barrier(acc))
    far = far_of(gradients(signal[:TWICE], ahead[:TWICE], ahead[TWICE:]))
    d_gates = gradients(past_both, signal[:TWICE], grad_out[:TWICE])
    first = grad_out[:TWICE].astype(jnp.float32) + contract_rows(d_gates, w_now)
    first = lax.optimization_barrier(first + far.astype(jnp.float32))
    mids = [acc + back.astype(jnp.float32) for acc, back in zip(accs[:-1], backs)]
    out = jnp.concatenate([first, *mids, accs[-1]], 0)
    last = accs[-1] + backs[-1].astype(jnp.float32)
    return lax.dynamic_update_slice(out, last, (cuts[-1][0], 0))


def solution(mesh):
    in_specs = (P("seq", None), P("seq", None), P(), P())
    out_specs = P("seq", None)
    return jax.shard_map(shards, mesh=mesh, in_specs=in_specs, out_specs=out_specs, check_vma=False)
```

```python
import functools

import jax
import jax.numpy as jnp
from jax import lax
from jax.experimental import pallas as pl
from jax.experimental.pallas import tpu as pltpu
from jax.sharding import PartitionSpec as P


PARTS = (400, 304)
TWICE = 320
COVER = 10**10


def from_behind(block, axis, distance):
    devices = range(lax.axis_size(axis))
    route = [(i - distance, i) for i in devices if i - distance in devices]
    return lax.ppermute(block, axis, route)


def contract_rows(left, right):
    return lax.dot_general(
        left, right, (((1,), (1,)), ((), ())), preferred_element_type=jnp.float32
    )


def cut_body(pieces, *refs):
    count = len(refs) - 1 - len({o for _, _, o, _, _ in pieces})
    sources, targets, sems = refs[:count], refs[count:-1], refs[-1]
    copies = []
    for k, (source, at, target, to, size) in enumerate(pieces):
        rows = sources[source].at[pl.ds(at, size)]
        copies.append(pltpu.make_async_copy(rows, targets[target].at[pl.ds(to, size)], sems.at[k]))
        copies[-1].start()
    for copy in copies:
        copy.wait()


def cut_rows(arrays, pieces, sizes, space, flops):
    width = arrays[0].shape[1]
    vmem = pl.BlockSpec(memory_space=pltpu.VMEM)
    return pl.pallas_call(
        functools.partial(cut_body, pieces),
        out_shape=[jax.ShapeDtypeStruct((n, width), arrays[0].dtype) for n in sizes],
        in_specs=[pl.BlockSpec(memory_space=space)] * len(arrays),
        out_specs=[vmem] * len(sizes),
        scratch_shapes=[pltpu.SemaphoreType.DMA((len(pieces),))],
        cost_estimate=pl.CostEstimate(flops=flops, bytes_accessed=0, transcendentals=0),
        compiler_params=pltpu.CompilerParams(vmem_limit_bytes=2 * 2**20),
    )(*arrays)


def shards(signal, grad_out, conv_weight, proj_weight):
    _, width = signal.shape
    w_past = conv_weight[:width]
    w_now = conv_weight[width:]

    def gradients(past, now, grad):
        own = jnp.dot(now, w_now, preferred_element_type=jnp.float32)
        gates = own + jnp.dot(past, w_past, preferred_element_type=jnp.float32)
        tanh_part = jnp.tanh(gates[:, :width])
        sig_part = jax.nn.sigmoid(gates[:, width:])
        d_mixed = contract_rows(grad, proj_weight)
        d_tanh = d_mixed * sig_part * (1.0 - tanh_part * tanh_part)
        d_sig = d_mixed * tanh_part * sig_part * (1.0 - sig_part)
        return jnp.concatenate([d_tanh, d_sig], 1).astype(jnp.bfloat16)

    def far_of(d_gates):
        return contract_rows(d_gates, w_past).astype(jnp.bfloat16)

    cuts = [(TWICE + sum(PARTS[:k]), TWICE + sum(PARTS[: k + 1])) for k in range(len(PARTS))]
    pieces = ((0, TWICE, 0, 0, PARTS[0]), (0, 0, 1, 0, TWICE), (1, 0, 1, TWICE, TWICE))
    held = [pltpu.with_memory_space_constraint(a, pltpu.HBM) for a in (signal, grad_out)]
    part, both = cut_rows(held, pieces, (PARTS[0], 2 * TWICE), pltpu.HBM, 0)
    past = [from_behind(part, "seq", 2)]
    ahead = from_behind(both, "seq", -2)
    pieces = ((0, cuts[1][0], 0, 0, PARTS[1]), (0, 0, 1, 0, TWICE))
    part, head = cut_rows([signal, grad_out], pieces, (PARTS[1], TWICE), pltpu.VMEM, COVER)
    past.append(from_behind(part, "seq", 2))
    past_both = from_behind(head, "seq", 2)
    accs = []
    backs = []
    for k, (a, b) in enumerate(cuts):
        d_gates = gradients(past[k], signal[a:b], grad_out[a:b])
        backs.append(from_behind(far_of(d_gates), "seq", -2))
        acc = grad_out[a:b].astype(jnp.float32) + contract_rows(d_gates, w_now)
        accs.append(lax.optimization_barrier(acc))
    far = far_of(gradients(signal[:TWICE], ahead[:TWICE], ahead[TWICE:]))
    d_gates = gradients(past_both, signal[:TWICE], grad_out[:TWICE])
    first = grad_out[:TWICE].astype(jnp.float32) + contract_rows(d_gates, w_now)
    first = lax.optimization_barrier(first + far.astype(jnp.float32))
    mids = [acc + back.astype(jnp.float32) for acc, back in zip(accs[:-1], backs)]
    out = jnp.concatenate([first, *mids, accs[-1]], 0)
    last = accs[-1] + backs[-1].astype(jnp.float32)
    return lax.dynamic_update_slice(out, last, (cuts[-1][0], 0))


def solution(mesh):
    in_specs = (P("seq", None), P("seq", None), P(), P())
    out_specs = P("seq", None)
    return jax.shard_map(shards, mesh=mesh, in_specs=in_specs, out_specs=out_specs, check_vma=False)
```
